32 devices in a mesh: layer: 4 (over x, core), ex: 8 (over z, y).
Axes of the slice: x: 2, y: 2, z: 4, core: 2. Of those that a mesh axis runs over, the one named last changes fastest.
Arguments:
- queries: bfloat16 [128, 8, 4096], P('ex', 'layer'), may hold values from -6 to 6
- stored: bfloat16 [2048, 8, 4096], P('ex', 'layer'), may hold values from -0.03125 to 0.03125
- left_inv: bfloat16 [8, 64, 64], P('layer'), may hold values from -0.078125 to 2
- right_inv: bfloat16 [8, 64, 64], P('layer'), may hold values from -0.078125 to 2
Outputs:
- scores: float32 [128, 2048], P('layer', 'ex')
The draws below stay inside these ranges and needn't reach their ends.
All inputs are finite; a program needn't handle non-finite values.
Results may differ from the reference program's by a relative error of at most 0.0041.
Values may be sent and summed in bfloat16 or wider, within the bound.
A program may use at most 128 MiB of HBM per device.

```python
import jax
import jax.numpy as jnp
from jax import lax

SIDE = 64
LAYERS = 8
STORED = 2048
QUERIES = 128


def factor_draw(key):
    keys = jax.random.split(key, 2)
    edge = 0.078125
    diag_vals = jnp.exp(jax.random.uniform(keys[0], (LAYERS, SIDE), jnp.float32, jnp.log(0.5), jnp.log(2.0)))
    diag_vals = diag_vals.at[:, 0].set(2.0)
    offdiag = jax.random.normal(keys[1], (LAYERS, SIDE, SIDE), jnp.float32) * 0.03
    offdiag = jnp.clip(offdiag, -edge, edge)
    offdiag = offdiag.at[:, 0, 1].set(-edge)
    eye = jnp.eye(SIDE, dtype=jnp.float32)
    return offdiag * (1.0 - eye) + eye * diag_vals[:, :, None]


def draw_left_inv(key, part):
    return factor_draw(jax.random.fold_in(key, 11)).astype(jnp.bfloat16)


def draw_right_inv(key, part):
    return factor_draw(jax.random.fold_in(key, 23)).astype(jnp.bfloat16)


def spiked(array, rng, source, target, parts, factor):
    owner, partner = [(jnp.arange(array.shape[axis_at]) // (array.shape[axis_at] // parts)).reshape([-1 if axis == axis_at else 1 for axis in range(array.ndim)]) for axis_at in (source, target)]
    chosen = jax.random.permutation(rng, parts)[partner]
    strong = (owner == chosen) | (owner == (partner + parts // 2) % parts)
    return jnp.where(strong, factor * array, array)


def shard_levels(stream_key, dims, shards, least, high):
    level, own = 1.0, jax.random.fold_in(stream_key, 6)
    for axis_at, shards_of in shards:
        steps = jnp.exp(jax.random.uniform(jax.random.fold_in(own, axis_at), (shards_of,), jnp.float32, least / len(shards), high / len(shards)))
        level = level * jnp.repeat(steps, dims[axis_at] // shards_of).reshape([-1 if axis == axis_at else 1 for axis in range(len(dims))])
    return level


def scatter_about(own_key, shape, width, reach, pieces=(), held_as=jnp.bfloat16):
    result = width * jax.random.normal(own_key, shape, jnp.float32)
    if pieces:
        result = result * shard_levels(own_key, shape, pieces, -0.22, 0.18)
    return jnp.clip(result, -reach, reach).astype(held_as)


def noise_with(rng, extent, spread, reach, cuts, heavy, kind=jnp.bfloat16):
    values = spread * jax.random.normal(rng, extent, jnp.float32)
    if cuts:
        values = values * shard_levels(rng, extent, cuts, -0.22, 0.18)
    return jnp.clip(spiked(values, jax.random.fold_in(rng, 3), *heavy), -reach, reach).astype(kind)


def setup_inputs(seed: int = 0) -> dict:
    arg_keys = jax.random.split(jax.random.key(seed), 5)
    return {
        "queries": noise_with(arg_keys[0], (QUERIES, LAYERS, SIDE * SIDE), 1.0, 6.0, ((0, 8), (1, 4)), (1, 0, 8, 2.0)),
        "stored": scatter_about(arg_keys[1], (STORED, LAYERS, SIDE * SIDE), (LAYERS * SIDE * SIDE) ** -0.5, 0.03125, ((0, 8), (1, 4))),
        "left_inv": draw_left_inv(jax.random.fold_in(arg_keys[4], 71), 0),
        "right_inv": draw_right_inv(jax.random.fold_in(arg_keys[4], 71), 0),
    }


def precondition(grads, left_fac, right_fac):
    mats = grads.reshape(grads.shape[0], SIDE, SIDE).astype(jnp.float32)
    left_side = jnp.einsum("ia,qaj->qij", left_fac.astype(jnp.float32), mats).astype(jnp.bfloat16)
    ready = jnp.einsum("qib,bj->qij", left_side.astype(jnp.float32), right_fac.astype(jnp.float32)).astype(jnp.bfloat16)
    return ready.reshape(grads.shape[0], SIDE * SIDE)


def reference(queries, stored, left_inv, right_inv):
    def layer_step(index, total):
        grads = lax.dynamic_index_in_dim(queries, index, 1, keepdims=False)
        column = lax.dynamic_index_in_dim(stored, index, 1, keepdims=False)
        left_fac = lax.dynamic_index_in_dim(left_inv, index, 0, keepdims=False)
        right_fac = lax.dynamic_index_in_dim(right_inv, index, 0, keepdims=False)
        ready = precondition(grads, left_fac, right_fac)
        return total + jnp.dot(ready, column.T, preferred_element_type=jnp.float32)

    start = jnp.zeros((QUERIES, STORED), jnp.float32)
    return lax.fori_loop(0, LAYERS, layer_step, start)
```

```python
import functools

import jax
import jax.numpy as jnp
from jax import lax
from jax.experimental import pallas as pl
from jax.experimental.pallas import tpu as pltpu
from jax.sharding import PartitionSpec as P

MESH = pl.DeviceIdType.MESH
LANES = 128
F32 = jnp.float32
BF16 = jnp.bfloat16


def iota(shape, axis):
    return lax.broadcasted_iota(jnp.int32, shape, axis)


def one_hot(mask):
    return jnp.where(mask, 1.0, 0.0).astype(BF16)


def dot(a, b):
    return jnp.dot(a, b, preferred_element_type=F32)


def kernel(
    groups, ex, per_block, layers_here, side, parts,
    q_hbm, s_hbm, l_ref, r_ref, out_ref,
    gathered, raw, flat_stored, lifted, left_mat, right_mat, ready_wide, ready_flat,
    partial, arrived,
    got, sent_up, sent_down, sent_across, own_sem, raw_sem, out_sem, in_sem,
):
    layer = lax.axis_index("layer")
    me = lax.axis_index("ex")
    depth = ex // 2
    z, y = me // 2, me % 2
    per = LANES // side
    tiles = side // per
    rows = tiles * layers_here
    piece = per_block // parts

    barrier = pltpu.get_barrier_semaphore()

    def greet(**where):
        pl.semaphore_signal(barrier, inc=1, device_id=where, device_id_type=MESH)

    pl.when(z > 0)(lambda: greet(ex=me - 2))
    pl.when(z < depth - 1)(lambda: greet(ex=me + 2))
    greet(ex=me + 1 - 2 * y)
    for step in range(1, groups):
        greet(layer=lax.rem(layer + step, groups))

    own_copy = pltpu.make_async_copy(q_hbm, gathered.at[me], own_sem)
    own_copy.start()
    n_raw = raw_sem.shape[0]
    stored_rows = raw.shape[0]
    raw_rows = stored_rows // n_raw

    def raw_copy(i):
        at = pl.ds(i * raw_rows, raw_rows)
        return pltpu.make_async_copy(s_hbm.at[at], raw.at[at], raw_sem.at[i])

    for i in range(n_raw):
        raw_copy(i).start()

    here = (z > 0).astype(jnp.int32) + (z < depth - 1).astype(jnp.int32)
    pl.semaphore_wait(barrier, here + groups)

    def hop(block, h, sem, target, source=None):
        at = pl.ds(h * piece, piece)
        return pltpu.make_async_remote_copy(
            src_ref=gathered.at[block, at] if source is None else source.at[at],
            dst_ref=gathered.at[block, at],
            send_sem=sem.at[block, h],
            recv_sem=got.at[block, h],
            device_id={"ex": target},
            device_id_type=MESH,
        )

    across = me + 1 - 2 * y
    for h in range(parts):
        pl.when(z < depth - 1)(lambda: hop(me, h, sent_up, me + 2, q_hbm).start())
        pl.when(z > 0)(lambda: hop(me, h, sent_down, me - 2, q_hbm).start())
        hop(me, h, sent_across, across, q_hbm).start()

    spread = one_hot(
        iota((side, side), 1) == (iota((side, side), 0) % tiles) * per + iota((side, side), 0) // tiles
    )
    wide = one_hot(iota((side, LANES), 1) % side == iota((side, LANES), 0))
    right_cols = []
    for l in range(layers_here):
        ordered = dot(spread, l_ref[l]).astype(BF16)
        for low in range(per):
            col = iota((side, rows), 1)
            pick = one_hot(
                jnp.logical_and(
                    col % layers_here == l, iota((side, rows), 0) == (col // layers_here) * per + low
                )
            )
            at = (l * per + low) * side
            left_mat[at : at + side, :] = dot(ordered, pick).astype(BF16)
        tiled = dot(r_ref[l], wide)
        stack = jnp.concatenate([tiled] * (per * layers_here), axis=0)
        keep = iota(stack.shape, 0) // side == l * per + iota(stack.shape, 1) // side
        right_mat[:, l * LANES : (l + 1) * LANES] = jnp.where(keep, stack, 0.0).astype(BF16)

    batch = lifted.shape[0] // rows

    def lift(i, carry):
        at = pl.multiple_of(i * batch, batch)
        lifted[...] = raw[pl.ds(at, batch)].reshape(batch * rows, LANES).astype(F32)
        for r in range(rows):
            flat_stored[pl.ds(at, batch), r * LANES : (r + 1) * LANES] = lifted[
                pl.ds(r, batch, stride=rows), :
            ].astype(BF16)
        return carry

    per_raw = raw_rows // batch
    for i in range(n_raw):
        raw_copy(i).wait()
        lax.fori_loop(i * per_raw, (i + 1) * per_raw, lift, 0)

    def precondition(block, slot):
        lanes = [gathered[block, i] for i in range(per_block)]
        product = dot(left_mat[...], jnp.concatenate(lanes, axis=1))
        low = iota((side, LANES), 1) < side
        low_half = iota((tiles, LANES), 1) < side
        stacked = []
        for i in range(per_block):
            halves = []
            for l in range(layers_here):
                mine = product[l * per * side : (l + 1) * per * side, i * LANES : (i + 1) * LANES]
                both = jnp.where(low, mine[:side], mine[side:])
                both = both + pltpu.roll(both, side, 1)
                halves.append(jnp.where(low_half, both[:tiles], both[tiles:]).astype(BF16))
            stacked.append(jnp.concatenate(halves, axis=1))
        ready = dot(jnp.concatenate(stacked, axis=0), right_mat[...])
        for l in range(layers_here):
            ready_wide[l] = ready[:, l * LANES : (l + 1) * LANES]
        for c in range(tiles):
            for l in range(layers_here):
                at = (c * layers_here + l) * LANES
                ready_flat[slot * per_block : (slot + 1) * per_block, at : at + LANES] = ready_wide[
                    l, pl.ds(c, per_block, stride=tiles), :
                ].astype(BF16)

    def share(to):
        return pltpu.make_async_remote_copy(
            src_ref=partial.at[to],
            dst_ref=arrived.at[layer],
            send_sem=out_sem.at[to],
            recv_sem=in_sem.at[layer],
            device_id={"layer": to},
            device_id_type=MESH,
        )

    def compute(zz):
        for h in range(parts):
            hop(zz * 2 + 1 - y, h, sent_across, across).wait_recv()
        precondition(zz * 2, 0)
        precondition(zz * 2 + 1, 1)
        partial[zz] = lax.dot_general(
            ready_flat[...], flat_stored[...], (((1,), (1,)), ((), ())), preferred_element_type=F32
        )
        pl.when(zz != layer)(lambda: share(zz).start())

    def relay(distance):
        for h in range(parts):

            @pl.when(z >= distance)
            def _():
                block = me - 2 * distance
                hop(block, h, sent_up, me).wait_recv()
                pl.when(z < depth - 1)(lambda: hop(block, h, sent_up, me + 2).start())
                hop(block, h, sent_across, across).start()

            @pl.when(z + distance < depth)
            def _():
                block = me + 2 * distance
                hop(block, h, sent_down, me).wait_recv()
                pl.when(z > 0)(lambda: hop(block, h, sent_down, me - 2).start())
                hop(block, h, sent_across, across).start()

    own_copy.wait()

    def turn(i, carry):
        distance = (i + 1) // 2
        zz = jnp.where(i % 2 == 1, z - distance, z + distance)

        @pl.when(i % 2 == 0)
        def _():
            pl.when(distance + 1 < depth)(lambda: relay(distance + 1))

        pl.when(jnp.logical_and(zz >= 0, zz < depth))(lambda: compute(zz))
        return carry

    lax.fori_loop(0, 2 * depth - 1, turn, 0)

    total = partial[layer]
    for step in range(1, groups):
        other = lax.rem(layer + step, groups)
        pltpu.make_async_remote_copy(
            src_ref=partial.at[other],
            dst_ref=arrived.at[other],
            send_sem=out_sem.at[other],
            recv_sem=in_sem.at[other],
            device_id={"layer": other},
            device_id_type=MESH,
        ).wait_recv()
        total = total + arrived[other]
    out_ref[...] = total

    for step in range(1, groups):
        share(lax.rem(layer + step, groups)).wait_send()

    def drain(zz, carry):
        block = zz * 2 + y
        for h in range(parts):
            hop(block, h, sent_across, across).wait_send()
            up = jnp.logical_and(zz <= z, z < depth - 1)
            down = jnp.logical_and(zz >= z, z > 0)
            pl.when(up)(lambda: hop(block, h, sent_up, me + 2).wait_send())
            pl.when(down)(lambda: hop(block, h, sent_down, me - 2).wait_send())
        return carry

    lax.fori_loop(0, depth, drain, 0)


def rows_of(array, side):
    count, layers_here, size = array.shape
    tiles = size // LANES
    split = array.reshape(count, layers_here, tiles, LANES).transpose(0, 2, 1, 3)
    return split.reshape(count, tiles * layers_here, LANES)


def shards(groups, ex, queries, stored, left_inv, right_inv):
    per_block, layers_here, size = queries.shape
    side = left_inv.shape[1]
    stored_rows = stored.shape[0]
    per = LANES // side
    rows = size // LANES * layers_here
    parts = 2
    batch = 16
    n_raw = 4
    dma = pltpu.SemaphoreType.DMA
    return pl.pallas_call(
        functools.partial(kernel, groups, ex, per_block, layers_here, side, parts),
        out_shape=jax.ShapeDtypeStruct((2 * per_block, stored_rows), F32),
        in_specs=[pl.BlockSpec(memory_space=pl.ANY)] * 2 + [pl.BlockSpec(memory_space=pltpu.VMEM)] * 2,
        out_specs=pl.BlockSpec(memory_space=pltpu.VMEM),
        scratch_shapes=[
            pltpu.VMEM((ex, per_block, rows, LANES), BF16),
            pltpu.VMEM((stored_rows, rows, LANES), BF16),
            pltpu.VMEM((stored_rows, rows * LANES), BF16),
            pltpu.VMEM((batch * rows, LANES), F32),
            pltpu.VMEM((layers_here * per * side, rows), BF16),
            pltpu.VMEM((layers_here * LANES, layers_here * LANES), BF16),
            pltpu.VMEM((layers_here, per_block * size // LANES, LANES), F32),
            pltpu.VMEM((2 * per_block, rows * LANES), BF16),
            pltpu.VMEM((groups, 2 * per_block, stored_rows), F32),
            pltpu.VMEM((groups, 2 * per_block, stored_rows), F32),
            dma((ex, parts)),
            dma((ex, parts)),
            dma((ex, parts)),
            dma((ex, parts)),
            dma,
            dma((n_raw,)),
            dma((groups,)),
            dma((groups,)),
        ],
        compiler_params=pltpu.CompilerParams(
            collective_id=0, has_side_effects=True, vmem_limit_bytes=60 << 20
        ),
    )(rows_of(queries, side), rows_of(stored, side), left_inv, right_inv)


def solution(mesh):
    placed = (
        P("ex", "layer", None),
        P("ex", "layer", None),
        P("layer", None, None),
        P("layer", None, None),
    )
    groups, ex = mesh.shape["layer"], mesh.shape["ex"]
    return jax.shard_map(
        functools.partial(shards, groups, ex),
        mesh=mesh, in_specs=placed, out_specs=P("layer", "ex"), check_vma=False,
    )
```

```python
import functools

import jax
import jax.numpy as jnp
from jax import lax
from jax.experimental import pallas as pl
from jax.experimental.pallas import tpu as pltpu
from jax.sharding import PartitionSpec as P

MESH = pl.DeviceIdType.MESH
LANES = 128
F32 = jnp.float32
BF16 = jnp.bfloat16


def iota(shape, axis):
    return lax.broadcasted_iota(jnp.int32, shape, axis)


def one_hot(mask):
    return jnp.where(mask, 1.0, 0.0).astype(BF16)


def dot(a, b):
    return jnp.dot(a, b, preferred_element_type=F32)


def kernel(
    groups, ex, per_block, layers_here, side, cuts, batch,
    q_hbm, s_hbm, l_ref, r_ref, out_ref,
    gathered, raw, flat_stored, left_mat, right_mat, ready_flat,
    partial, arrived,
    got, sent_up, sent_down, sent_across, own_sem, raw_sem, out_sem, in_sem,
):
    layer = lax.axis_index("layer")
    me = lax.axis_index("ex")
    depth = ex // 2
    z, y = me // 2, me % 2
    per = LANES // side
    tiles = side // per
    rows = tiles * layers_here
    parts = len(cuts) - 1
    last = parts - 1

    barrier = pltpu.get_barrier_semaphore()

    def greet(**where):
        pl.semaphore_signal(barrier, inc=1, device_id=where, device_id_type=MESH)

    pl.when(z > 0)(lambda: greet(ex=me - 2))
    pl.when(z < depth - 1)(lambda: greet(ex=me + 2))
    greet(ex=me + 1 - 2 * y)
    for step in range(1, groups):
        greet(layer=lax.rem(layer + step, groups))

    own_copy = pltpu.make_async_copy(q_hbm, gathered.at[me], own_sem)
    own_copy.start()
    n_raw = raw_sem.shape[0]
    stored_rows = raw.shape[0]
    raw_rows = stored_rows // n_raw

    def raw_copy(i):
        at = pl.ds(i * raw_rows, raw_rows)
        return pltpu.make_async_copy(s_hbm.at[at], raw.at[at], raw_sem.at[i])

    for i in range(n_raw):
        raw_copy(i).start()

    here = (z > 0).astype(jnp.int32) + (z < depth - 1).astype(jnp.int32)
    pl.semaphore_wait(barrier, here + groups)

    def hop(block, h, sem, target, source=None):
        at = pl.ds(cuts[h], cuts[h + 1] - cuts[h])
        return pltpu.make_async_remote_copy(
            src_ref=gathered.at[block, at] if source is None else source.at[at],
            dst_ref=gathered.at[block, at],
            send_sem=sem.at[block, h],
            recv_sem=got.at[block, h],
            device_id={"ex": target},
            device_id_type=MESH,
        )

    across = me + 1 - 2 * y
    hop(me, last, sent_across, across, q_hbm).start()
    for h in range(parts):
        pl.when(z < depth - 1)(lambda: hop(me, h, sent_up, me + 2, q_hbm).start())
        pl.when(z > 0)(lambda: hop(me, h, sent_down, me - 2, q_hbm).start())
        if h < last:
            hop(me, h, sent_across, across, q_hbm).start()

    spread = one_hot(
        iota((side, side), 1) == (iota((side, side), 0) % tiles) * per + iota((side, side), 0) // tiles
    )
    wide = one_hot(iota((side, LANES), 1) % side == iota((side, LANES), 0))
    right_cols = []
    for l in range(layers_here):
        ordered = dot(spread, l_ref[l]).astype(BF16)
        for low in range(per):
            col = iota((side, rows), 1)
            pick = one_hot(
                jnp.logical_and(
                    col % layers_here == l, iota((side, rows), 0) == (col // layers_here) * per + low
                )
            )
            at = (l * per + low) * side
            left_mat[at : at + side, :] = dot(ordered, pick).astype(BF16)
        tiled = dot(r_ref[l], wide)
        stack = jnp.concatenate([tiled] * (per * layers_here), axis=0)
        keep = iota(stack.shape, 0) // side == l * per + iota(stack.shape, 1) // side
        right_mat[:, l * LANES : (l + 1) * LANES] = jnp.where(keep, stack, 0.0).astype(BF16)


    def lift(i, carry):
        at = pl.multiple_of(i * batch, batch)
        turned = jnp.swapaxes(raw[pl.ds(at, batch)], 0, 1)
        for r in range(rows):
            flat_stored[pl.ds(at, batch), r * LANES : (r + 1) * LANES] = turned[r]
        return carry

    per_raw = raw_rows // batch
    for i in range(n_raw):
        raw_copy(i).wait()
        lax.fori_loop(i * per_raw, (i + 1) * per_raw, lift, 0)

    def precondition(block, slot):
        lanes = [gathered[block, i] for i in range(per_block)]
        product = dot(left_mat[...], jnp.concatenate(lanes, axis=1))
        low = iota((side, LANES), 1) < side
        low_half = iota((tiles, LANES), 1) < side
        stacked = []
        for i in range(per_block):
            halves = []
            for l in range(layers_here):
                mine = product[l * per * side : (l + 1) * per * side, i * LANES : (i + 1) * LANES]
                both = jnp.where(low, mine[:side], mine[side:])
                both = both + pltpu.roll(both, side, 1)
                halves.append(jnp.where(low_half, both[:tiles], both[tiles:]).astype(BF16))
            stacked.append(jnp.concatenate(halves, axis=1))
        ready = dot(jnp.concatenate(stacked, axis=0), right_mat[...])
        wide_at = layers_here * LANES
        turned = jnp.swapaxes(ready.astype(BF16).reshape(per_block, tiles, wide_at), 0, 1)
        for c in range(tiles):
            ready_flat[slot * per_block : (slot + 1) * per_block, c * wide_at : (c + 1) * wide_at] = turned[c]

    def share(to):
        return pltpu.make_async_remote_copy(
            src_ref=partial.at[to],
            dst_ref=arrived.at[layer],
            send_sem=out_sem.at[to],
            recv_sem=in_sem.at[layer],
            device_id={"layer": to},
            device_id_type=MESH,
        )

    def compute(zz):
        precondition(zz * 2 + y, 0)
        other = zz * 2 + 1 - y
        for h in range(parts):
            if h < last:
                hop(other, h, sent_across, across).wait_recv()
        precondition(other, 1)
        scores = lax.dot_general(
            ready_flat[...], flat_stored[...], (((1,), (1,)), ((), ())), preferred_element_type=F32
        )
        partial[zz, pl.ds(pl.multiple_of(y * per_block, per_block), per_block)] = scores[:per_block]
        partial[zz, pl.ds(pl.multiple_of((1 - y) * per_block, per_block), per_block)] = scores[per_block:]
        pl.when(zz != layer)(lambda: share(zz).start())

    def onward(block, h, upward):
        if upward:
            pl.when(z < depth - 1)(lambda: hop(block, h, sent_up, me + 2).start())
        else:
            pl.when(z > 0)(lambda: hop(block, h, sent_down, me - 2).start())

    def relay(distance):
        for h in range(parts + 1):
            for upward in (True, False):

                @pl.when(z >= distance if upward else z + distance < depth)
                def _():
                    offset = -2 * distance if upward else 2 * distance
                    block = (me if h < parts else across) + offset
                    piece = min(h, last)
                    hop(block, piece, sent_up, me).wait_recv()
                    onward(block, piece, upward)
                    if h < last:
                        hop(block, h, sent_across, across).start()

    hop(across, last, sent_across, across).wait_recv()
    onward(across, last, True)
    onward(across, last, False)
    own_copy.wait()

    def turn(i, carry):
        distance = (i + 1) // 2
        zz = jnp.where(i % 2 == 1, z - distance, z + distance)

        @pl.when(jnp.logical_or(i == 0, i % 2 == 1))
        def _():
            pl.when(distance + 1 < depth)(lambda: relay(distance + 1))

        pl.when(jnp.logical_and(zz >= 0, zz < depth))(lambda: compute(zz))
        return carry

    lax.fori_loop(0, 2 * depth - 1, turn, 0)

    total = partial[layer]
    for step in range(1, groups):
        other = lax.rem(layer + step, groups)
        pltpu.make_async_remote_copy(
            src_ref=partial.at[other],
            dst_ref=arrived.at[other],
            send_sem=out_sem.at[other],
            recv_sem=in_sem.at[other],
            device_id={"layer": other},
            device_id_type=MESH,
        ).wait_recv()
        total = total + arrived[other]
    out_ref[...] = total

    for step in range(1, groups):
        share(lax.rem(layer + step, groups)).wait_send()

    def drain(zz, carry):
        up = jnp.logical_and(zz <= z, z < depth - 1)
        down = jnp.logical_and(zz >= z, z > 0)
        for h in range(parts + 1):
            block = zz * 2 + (y if h < parts else 1 - y)
            piece = min(h, last)
            if h < last:
                hop(block, h, sent_across, across).wait_send()
            pl.when(up)(lambda: hop(block, piece, sent_up, me + 2).wait_send())
            pl.when(down)(lambda: hop(block, piece, sent_down, me - 2).wait_send())
        return carry

    lax.fori_loop(0, depth, drain, 0)
    hop(me, last, sent_across, across).wait_send()


def rows_of(array, side):
    count, layers_here, size = array.shape
    tiles = size // LANES
    split = array.reshape(count, layers_here, tiles, LANES).transpose(0, 2, 1, 3)
    return split.reshape(count, tiles * layers_here, LANES)


def shards(groups, ex, queries, stored, left_inv, right_inv):
    per_block, layers_here, size = queries.shape
    side = left_inv.shape[1]
    stored_rows = stored.shape[0]
    per = LANES // side
    rows = size // LANES * layers_here
    detour = max(1, per_block * 3 // 16)
    cuts = (0, (per_block - detour + 1) // 2, per_block - detour, per_block)
    parts = len(cuts) - 1
    batch = 16
    n_raw = 4
    dma = pltpu.SemaphoreType.DMA
    return pl.pallas_call(
        functools.partial(kernel, groups, ex, per_block, layers_here, side, cuts, batch),
        out_shape=jax.ShapeDtypeStruct((2 * per_block, stored_rows), F32),
        in_specs=[pl.BlockSpec(memory_space=pl.ANY)] * 2 + [pl.BlockSpec(memory_space=pltpu.VMEM)] * 2,
        out_specs=pl.BlockSpec(memory_space=pltpu.VMEM),
        scratch_shapes=[
            pltpu.VMEM((ex, per_block, rows, LANES), BF16),
            pltpu.VMEM((stored_rows, rows, LANES), BF16),
            pltpu.VMEM((stored_rows, rows * LANES), BF16),
            pltpu.VMEM((layers_here * per * side, rows), BF16),
            pltpu.VMEM((layers_here * LANES, layers_here * LANES), BF16),
            pltpu.VMEM((2 * per_block, rows * LANES), BF16),
            pltpu.VMEM((groups, 2 * per_block, stored_rows), F32),
            pltpu.VMEM((groups, 2 * per_block, stored_rows), F32),
            dma((ex, parts)),
            dma((ex, parts)),
            dma((ex, parts)),
            dma((ex, parts)),
            dma,
            dma((n_raw,)),
            dma((groups,)),
            dma((groups,)),
        ],
        compiler_params=pltpu.CompilerParams(
            collective_id=0, has_side_effects=True, vmem_limit_bytes=60 << 20
        ),
    )(rows_of(queries, side), rows_of(stored, side), left_inv, right_inv)


def solution(mesh):
    placed = (
        P("ex", "layer", None),
        P("ex", "layer", None),
        P("layer", None, None),
        P("layer", None, None),
    )
    groups, ex = mesh.shape["layer"], mesh.shape["ex"]
    return jax.shard_map(
        functools.partial(shards, groups, ex),
        mesh=mesh, in_specs=placed, out_specs=P("layer", "ex"), check_vma=False,
    )
```

```python
import functools

import jax
import jax.numpy as jnp
from jax import lax
from jax.experimental import pallas as pl
from jax.experimental.pallas import tpu as pltpu
from jax.sharding import PartitionSpec as P

MESH = pl.DeviceIdType.MESH
LANES = 128
F32 = jnp.float32
BF16 = jnp.bfloat16


def iota(shape, axis):
    return lax.broadcasted_iota(jnp.int32, shape, axis)


def one_hot(mask):
    return jnp.where(mask, 1.0, 0.0).astype(BF16)


def dot(a, b):
    return jnp.dot(a, b, preferred_element_type=F32)


def kernel(
    groups, ex, per_block, layers_here, side, cuts, batch,
    q_hbm, s_hbm, l_ref, r_ref, out_ref,
    gathered, raw, flat_stored, left_mat, right_mat, ready_flat,
    partial, arrived,
    got, sent_up, sent_down, sent_across, own_sem, raw_sem, out_sem, in_sem,
):
    layer = lax.axis_index("layer")
    me = lax.axis_index("ex")
    depth = ex // 2
    z, y = me // 2, me % 2
    per = LANES // side
    tiles = side // per
    rows = tiles * layers_here
    parts = len(cuts) - 1
    last = parts - 1

    barrier = pltpu.get_barrier_semaphore()

    def greet(**where):
        pl.semaphore_signal(barrier, inc=1, device_id=where, device_id_type=MESH)

    pl.when(z > 0)(lambda: greet(ex=me - 2))
    pl.when(z < depth - 1)(lambda: greet(ex=me + 2))
    greet(ex=me + 1 - 2 * y)
    for step in range(1, groups):
        greet(layer=lax.rem(layer + step, groups))

    own_copy = pltpu.make_async_copy(q_hbm, gathered.at[me], own_sem)
    own_copy.start()
    n_raw = raw_sem.shape[0]
    stored_rows = raw.shape[0]
    raw_rows = stored_rows // n_raw

    def raw_copy(i):
        at = pl.ds(i * raw_rows, raw_rows)
        return pltpu.make_async_copy(s_hbm.at[at], raw.at[at], raw_sem.at[i])

    for i in range(n_raw):
        raw_copy(i).start()

    here = (z > 0).astype(jnp.int32) + (z < depth - 1).astype(jnp.int32)
    pl.semaphore_wait(barrier, here + groups)

    def hop(block, h, sem, target, source=None):
        at = pl.ds(cuts[h], cuts[h + 1] - cuts[h])
        return pltpu.make_async_remote_copy(
            src_ref=gathered.at[block, at] if source is None else source.at[at],
            dst_ref=gathered.at[block, at],
            send_sem=sem.at[block, h],
            recv_sem=got.at[block, h],
            device_id={"ex": target},
            device_id_type=MESH,
        )

    across = me + 1 - 2 * y
    hop(me, last, sent_across, across, q_hbm).start()
    for h in range(parts):
        pl.when(z < depth - 1)(lambda: hop(me, h, sent_up, me + 2, q_hbm).start())
        pl.when(z > 0)(lambda: hop(me, h, sent_down, me - 2, q_hbm).start())
        if h < last:
            hop(me, h, sent_across, across, q_hbm).start()

    spread = one_hot(
        iota((side, side), 1) == (iota((side, side), 0) % tiles) * per + iota((side, side), 0) // tiles
    )
    wide = one_hot(iota((side, LANES), 1) % side == iota((side, LANES), 0))
    right_cols = []
    for l in range(layers_here):
        ordered = dot(spread, l_ref[l]).astype(BF16)
        for low in range(per):
            col = iota((side, rows), 1)
            pick = one_hot(
                jnp.logical_and(
                    col % layers_here == l, iota((side, rows), 0) == (col // layers_here) * per + low
                )
            )
            at = (l * per + low) * side
            left_mat[at : at + side, :] = dot(ordered, pick).astype(BF16)
        tiled = dot(r_ref[l], wide)
        stack = jnp.concatenate([tiled] * (per * layers_here), axis=0)
        keep = iota(stack.shape, 0) // side == l * per + iota(stack.shape, 1) // side
        right_mat[:, l * LANES : (l + 1) * LANES] = jnp.where(keep, stack, 0.0).astype(BF16)


    def lift(i, carry):
        at = pl.multiple_of(i * batch, batch)
        turned = jnp.swapaxes(raw[pl.ds(at, batch)], 0, 1)
        for r in range(rows):
            flat_stored[pl.ds(at, batch), r * LANES : (r + 1) * LANES] = turned[r]
        return carry

    per_raw = raw_rows // batch
    for i in range(n_raw):
        raw_copy(i).wait()
        lax.fori_loop(i * per_raw, (i + 1) * per_raw, lift, 0)

    def precondition(block, slot, ready_flat):
        lanes = [gathered[block, i] for i in range(per_block)]
        product = dot(left_mat[...], jnp.concatenate(lanes, axis=1))
        low = iota((side, LANES), 1) < side
        low_half = iota((tiles, LANES), 1) < side
        stacked = []
        for i in range(per_block):
            halves = []
            for l in range(layers_here):
                mine = product[l * per * side : (l + 1) * per * side, i * LANES : (i + 1) * LANES]
                both = jnp.where(low, mine[:side], mine[side:])
                both = both + pltpu.roll(both, side, 1)
                halves.append(jnp.where(low_half, both[:tiles], both[tiles:]).astype(BF16))
            stacked.append(jnp.concatenate(halves, axis=1))
        ready = dot(jnp.concatenate(stacked, axis=0), right_mat[...])
        wide_at = layers_here * LANES
        turned = jnp.swapaxes(ready.astype(BF16).reshape(per_block, tiles, wide_at), 0, 1)
        for c in range(tiles):
            ready_flat[slot * per_block : (slot + 1) * per_block, c * wide_at : (c + 1) * wide_at] = turned[c]

    def share(to):
        return pltpu.make_async_remote_copy(
            src_ref=partial.at[to],
            dst_ref=arrived.at[layer],
            send_sem=out_sem.at[to],
            recv_sem=in_sem.at[layer],
            device_id={"layer": to},
            device_id_type=MESH,
        )

    def work(stage, zz, flat):
        other = zz * 2 + 1 - y
        if stage == 0:
            precondition(zz * 2 + y, 0, flat)
        elif stage == 1:
            for h in range(last):
                hop(other, h, sent_across, across).wait_recv()
            precondition(other, 1, flat)
        elif stage == 2:
            scores = lax.dot_general(
                flat[...], flat_stored[...], (((1,), (1,)), ((), ())), preferred_element_type=F32
            )
            partial[zz, pl.ds(pl.multiple_of(y * per_block, per_block), per_block)] = scores[:per_block]
            partial[zz, pl.ds(pl.multiple_of((1 - y) * per_block, per_block), per_block)] = scores[per_block:]
            pl.when(zz != layer)(lambda: share(zz).start())

    def onward(block, h, upward):
        if upward:
            pl.when(z < depth - 1)(lambda: hop(block, h, sent_up, me + 2).start())
        else:
            pl.when(z > 0)(lambda: hop(block, h, sent_down, me - 2).start())

    def relay(h, distance):
        for upward in (True, False):

            @pl.when(z >= distance if upward else z + distance < depth)
            def _():
                offset = -2 * distance if upward else 2 * distance
                block = (me if h < parts else across) + offset
                piece = min(h, last)
                hop(block, piece, sent_up, me).wait_recv()
                onward(block, piece, upward)
                if h < last:
                    hop(block, h, sent_across, across).start()

    hop(across, last, sent_across, across).wait_recv()
    onward(across, last, True)
    onward(across, last, False)
    own_copy.wait()

    def turn(distance, carry):
        below = z >= distance
        above = jnp.logical_and(distance > 0, z + distance < depth)
        for h in range(parts + 1):
            relay(h, distance + 1)
            pl.when(below)(lambda: work(h, z - distance, ready_flat.at[0]))
            pl.when(above)(lambda: work(h, z + distance, ready_flat.at[1]))
        return carry

    lax.fori_loop(0, depth, turn, 0)

    total = partial[layer]
    for step in range(1, groups):
        other = lax.rem(layer + step, groups)
        pltpu.make_async_remote_copy(
            src_ref=partial.at[other],
            dst_ref=arrived.at[other],
            send_sem=out_sem.at[other],
            recv_sem=in_sem.at[other],
            device_id={"layer": other},
            device_id_type=MESH,
        ).wait_recv()
        total = total + arrived[other]
    out_ref[...] = total

    for step in range(1, groups):
        share(lax.rem(layer + step, groups)).wait_send()

    def drain(zz, carry):
        up = jnp.logical_and(zz <= z, z < depth - 1)
        down = jnp.logical_and(zz >= z, z > 0)
        for h in range(parts + 1):
            block = zz * 2 + (y if h < parts else 1 - y)
            piece = min(h, last)
            if h < last:
                hop(block, h, sent_across, across).wait_send()
            pl.when(up)(lambda: hop(block, piece, sent_up, me + 2).wait_send())
            pl.when(down)(lambda: hop(block, piece, sent_down, me - 2).wait_send())
        return carry

    lax.fori_loop(0, depth, drain, 0)
    hop(me, last, sent_across, across).wait_send()


def rows_of(array, side):
    count, layers_here, size = array.shape
    tiles = size // LANES
    split = array.reshape(count, layers_here, tiles, LANES).transpose(0, 2, 1, 3)
    return split.reshape(count, tiles * layers_here, LANES)


def shards(groups, ex, queries, stored, left_inv, right_inv):
    per_block, layers_here, size = queries.shape
    side = left_inv.shape[1]
    stored_rows = stored.shape[0]
    per = LANES // side
    rows = size // LANES * layers_here
    detour = max(1, per_block // 8)
    cuts = (0, (per_block - detour + 1) // 2, per_block - detour, per_block)
    parts = len(cuts) - 1
    batch = 16
    n_raw = 4
    dma = pltpu.SemaphoreType.DMA
    return pl.pallas_call(
        functools.partial(kernel, groups, ex, per_block, layers_here, side, cuts, batch),
        out_shape=jax.ShapeDtypeStruct((2 * per_block, stored_rows), F32),
        in_specs=[pl.BlockSpec(memory_space=pl.ANY)] * 2 + [pl.BlockSpec(memory_space=pltpu.VMEM)] * 2,
        out_specs=pl.BlockSpec(memory_space=pltpu.VMEM),
        scratch_shapes=[
            pltpu.VMEM((ex, per_block, rows, LANES), BF16),
            pltpu.VMEM((stored_rows, rows, LANES), BF16),
            pltpu.VMEM((stored_rows, rows * LANES), BF16),
            pltpu.VMEM((layers_here * per * side, rows), BF16),
            pltpu.VMEM((layers_here * LANES, layers_here * LANES), BF16),
            pltpu.VMEM((2, 2 * per_block, rows * LANES), BF16),
            pltpu.VMEM((groups, 2 * per_block, stored_rows), F32),
            pltpu.VMEM((groups, 2 * per_block, stored_rows), F32),
            dma((ex, parts)),
            dma((ex, parts)),
            dma((ex, parts)),
            dma((ex, parts)),
            dma,
            dma((n_raw,)),
            dma((groups,)),
            dma((groups,)),
        ],
        compiler_params=pltpu.CompilerParams(
            collective_id=0, has_side_effects=True, vmem_limit_bytes=60 << 20
        ),
    )(rows_of(queries, side), rows_of(stored, side), left_inv, right_inv)


def solution(mesh):
    placed = (
        P("ex", "layer", None),
        P("ex", "layer", None),
        P("layer", None, None),
        P("layer", None, None),
    )
    groups, ex = mesh.shape["layer"], mesh.shape["ex"]
    return jax.shard_map(
        functools.partial(shards, groups, ex),
        mesh=mesh, in_specs=placed, out_specs=P("layer", "ex"), check_vma=False,
    )
```
